32 devices in a mesh: group: 2 (over x), chan: 16 (over z, y, core).
Axes of the slice: x: 2, y: 2, z: 4, core: 2. Of those that a mesh axis runs over, the one named last changes fastest.
Arguments:
- features: bfloat16 [384, 8, 12, 128], P('chan', 'group'), parts along dimension 1, may hold values from -10 to 10
- cache_one: bfloat16 [384, 4, 12, 128], P('chan', 'group'), parts along dimension 1, may hold values from -3 to 3
- cache_two: bfloat16 [384, 4, 12, 128], P('chan', 'group'), parts along dimension 1, may hold values from -3 to 3
- weight_one: bfloat16 [384, 10368], P('chan'), may hold values from -1 to 1
- bias_one: float32 [384], P('chan'), may hold values from -3 to 3
- gain_one: float32 [384], P('chan'), may hold values from 0.1 to 1.9
- weight_two: bfloat16 [384, 10368], P('chan'), may hold values from -0.078125 to 0.078125
- bias_two: float32 [384], P('chan'), may hold values from -3 to 3
- gain_two: float32 [384], P('chan'), may hold values from 0.1 to 1.9
Outputs:
- out_feats: bfloat16 [384, 8, 12, 128], P('chan', 'group'), parts along dimension 1
- next_one: bfloat16 [384, 4, 12, 128], P('chan', 'group'), parts along dimension 1
- next_two: bfloat16 [384, 4, 12, 128], P('chan', 'group'), parts along dimension 1
The draws below stay inside these ranges and needn't reach their ends.
There are 2 independent parts, one for each index of `group`. The reference program is written for one: setup_inputs(seed, part) draws one part's arguments, and reference() takes and returns one part's arrays. A program takes and returns all parts, laid end to end along the dimension named above; an argument that names none is the same for every part. Nothing has to cross between parts.
All inputs are finite; a program needn't handle non-finite values.
Results may differ from the reference program's by a relative error of at most 0.0095.
Values may be sent and summed in bfloat16 or wider, within the bound.
A program may use at most 128 MiB of HBM per device.

```python
import math
import jax
import jax.numpy as jnp
from jax import lax

C = 384
TF = 4
HT = 12
WT = 128


def draw_features(key, part):
    subkeys = jax.random.split(key, 3)
    channel_ramp = 3.0 ** (jnp.arange(C, dtype=jnp.float32) / C)
    chan_scale = 0.3 * channel_ramp * jnp.exp(jax.random.uniform(subkeys[0], (C,), jnp.float32, 0.0, math.log(3.4)))
    place_scale = jnp.exp(jax.random.uniform(subkeys[1], (TF, HT, WT), jnp.float32, math.log(0.1), 0.0))
    base_draw = jax.random.normal(subkeys[2], (C, TF, HT, WT), jnp.float32)
    base_draw = jnp.clip(base_draw, -3.0, 3.0)
    return (base_draw * chan_scale[:, None, None, None] * place_scale[None]).astype(jnp.bfloat16)


def draw_weight_one(key, part):
    subkeys = jax.random.split(key, 2)
    output_ramp = 3.0 ** (jnp.arange(C, dtype=jnp.float32) / C - 0.5)
    row_scale = output_ramp * jnp.exp(jax.random.uniform(subkeys[0], (C,), jnp.float32, 0.0, math.log(2.0)))
    values = jnp.clip(jax.random.normal(subkeys[1], (C, C, 27), jnp.float32), -3.0, 3.0)
    scaled = values * row_scale[None, :, None] / math.sqrt(27 * C)
    return scaled.reshape(C, C * 27).astype(jnp.bfloat16)


def strengthened(values, rng, source, target, shards_of, factor):
    owner, partner = [(jnp.arange(values.shape[axis_at]) // (values.shape[axis_at] // shards_of)).reshape([-1 if axis == axis_at else 1 for axis in range(values.ndim)]) for axis_at in (source, target)]
    chosen = jax.random.permutation(rng, shards_of)[partner]
    strong = (owner == chosen) | (owner == (partner + shards_of // 2) % shards_of)
    return jnp.where(strong, factor * values, values)


def block_levels(key, dims, cuts, least, top_value):
    gain = 1.0
    for position, blocks in cuts:
        heights = jax.random.uniform(jax.random.fold_in(jax.random.fold_in(key, 6), position), (blocks,), jnp.float32, least / len(cuts), top_value / len(cuts))
        gain = gain * jnp.repeat(jnp.exp(heights), dims[position] // blocks).reshape((-1,) + (1,) * (len(dims) - 1 - position))
    return gain


def scatter_about(rng, dims, deviation, most, cuts=(), kind=jnp.bfloat16):
    drawn = deviation * jax.random.normal(rng, dims, jnp.float32)
    if cuts:
        drawn = drawn * block_levels(rng, dims, cuts, -0.22, 0.18)
    return jnp.clip(drawn, -most, most).astype(kind)


def heavy_noise(rng, dims, scale, most, shards, heavy, held_as=jnp.bfloat16):
    entries = scale * jax.random.normal(rng, dims, jnp.float32)
    if shards:
        entries = entries * block_levels(rng, dims, shards, -0.22, 0.18)
    return jnp.clip(strengthened(entries, jax.random.fold_in(rng, 3), *heavy), -most, most).astype(held_as)


def setup_inputs(seed: int = 0, part: int = 0) -> dict:
    arg_keys = jax.random.split(jax.random.key(seed), 10)
    own_keys = jax.random.split(jax.random.fold_in(arg_keys[9], part), 10)
    return {
        "features": draw_features(jax.random.fold_in(jax.random.fold_in(arg_keys[9], part), 71), part),
        "cache_one": scatter_about(own_keys[1], (C, 2, HT, WT), 0.5, 3.0, ((0, 16),)),
        "cache_two": scatter_about(own_keys[2], (C, 2, HT, WT), 0.5, 3.0, ((0, 16),)),
        "weight_one": draw_weight_one(jax.random.fold_in(arg_keys[9], 71), part),
        "bias_one": scatter_about(arg_keys[4], (C,), 0.5, 3.0, ((0, 16),), jnp.float32),
        "gain_one": jnp.clip(1.0 + 0.18 * jax.random.normal(arg_keys[5], (C,), jnp.float32), 0.1, 1.9),
        "weight_two": heavy_noise(arg_keys[6], (C, 27 * C), (27 * C) ** -0.5, 0.078125, ((0, 16),), (0, 1, 16, 2.0)),
        "bias_two": scatter_about(arg_keys[7], (C,), 0.5, 3.0, ((0, 16),), jnp.float32),
        "gain_two": jnp.clip(1.0 + 0.18 * jax.random.normal(arg_keys[8], (C,), jnp.float32), 0.1, 1.9),
    }


def normalize(values, gain_row):
    floats = values.astype(jnp.float32)
    squares = lax.optimization_barrier(jnp.mean(floats * floats, axis=0))
    scaled = floats * lax.rsqrt(squares + 1e-06)[None] * gain_row[:, None, None, None]
    return jax.nn.silu(scaled).astype(jnp.bfloat16)

def convolve(stacked, weights, bias_row):
    channels = weights.shape[0]
    kernel = weights.astype(jnp.float32).reshape(channels, channels, 3, 3, 3).transpose(1, 0, 2, 3, 4)
    result = lax.conv_general_dilated(stacked.astype(jnp.float32)[None], kernel, (1, 1, 1), ((0, 0), (1, 1), (1, 1)), dimension_numbers=('NCDHW', 'OIDHW', 'NCDHW'), precision=lax.Precision.HIGHEST)
    return result[0] + bias_row[:, None, None, None]

def reference(features, cache_one, cache_two, weight_one, bias_one, gain_one, weight_two, bias_two, gain_two):
    active_one = normalize(features, gain_one)
    middle = convolve(jnp.concatenate((cache_one, active_one), axis=1), weight_one, bias_one).astype(jnp.bfloat16)
    active_two = normalize(middle, gain_two)
    branch = convolve(jnp.concatenate((cache_two, active_two), axis=1), weight_two, bias_two)
    output = (features.astype(jnp.float32) + branch).astype(jnp.bfloat16)
    frames = active_one.shape[1]
    return (output, active_one[:, frames - 2:], active_two[:, frames - 2:])
```

```python
import functools

import jax
import jax.numpy as jnp
from jax import lax
from jax.experimental import pallas as pl
from jax.experimental.pallas import tpu as pltpu
from jax.sharding import PartitionSpec as P

F32 = jnp.float32
BF16 = jnp.bfloat16


def kernel(
    d, feat, c1, c2, w1, w2, b1, g1, b2, g2, out, n1, n2,
    z, xc, part, recv, summed, last_recv, last_sum, mid, sq, sq_recv, send_sem, recv_sem, sq_send, sq_sem,
):
    n, L, C, Cl, Kp, T, H, W = d["n"], d["L"], d["C"], d["Cl"], d["Kp"], d["T"], d["H"], d["W"]
    hc, nh, nch, CH, halvings, rem, window = (
        d["hc"], d["nh"], d["nch"], d["CH"], d["halvings"], d["rem"], d["window"]
    )
    me = lax.axis_index("chan")
    bits = [lax.rem(me // (1 << k), 2) for k in range(L)]
    partner = [me + (1 << k) * (1 - 2 * bits[k]) for k in range(L)]

    barrier = pltpu.get_barrier_semaphore()
    for k in range(L):
        pl.semaphore_signal(
            barrier, inc=1, device_id={"chan": partner[k]}, device_id_type=pl.DeviceIdType.MESH
        )

    lane = lax.broadcasted_iota(jnp.int32, (Kp, W), 1)

    def put(cv, frame, h, x):
        at = pl.ds(pl.multiple_of((frame * (H + 2) + h + 1) * W, W), W)
        z[cv, 1, :, at] = x.astype(BF16)
        z[cv, 0, :, at] = jnp.where(lane == 0, 0.0, pltpu.roll(x, 1, 1)).astype(BF16)
        z[cv, 2, :, at] = jnp.where(lane == W - 1, 0.0, pltpu.roll(x, W - 1, 1)).astype(BF16)

    def row(r):
        return pl.ds(pl.multiple_of(r * W, W), W)

    @pl.loop(0, T * H)
    def _(r):
        x = feat[:, row(r)].astype(F32)
        sq[0, pl.ds(r, 1), :] = jnp.sum(x * x, axis=0, keepdims=True)

    pl.semaphore_wait(barrier, L)

    def sq_copy(cv, k):
        return pltpu.make_async_remote_copy(
            src_ref=sq.at[cv * (L + 1) + k],
            dst_ref=sq_recv.at[cv * L + k],
            send_sem=sq_send.at[cv * L + k],
            recv_sem=sq_sem.at[cv * L + k],
            device_id={"chan": partner[k]},
            device_id_type=pl.DeviceIdType.MESH,
        )

    def reduce_squares(cv, first_work):
        sq_copy(cv, 0).start()
        first_work()
        for k in range(L):
            sq_copy(cv, k).wait_recv()
            sq[cv * (L + 1) + k + 1] = sq[cv * (L + 1) + k] + sq_recv[cv * L + k]
            if k + 1 < L:
                sq_copy(cv, k + 1).start()
        for k in range(L):
            sq_copy(cv, k).wait_send()

    def caches():
        for cv, cache in ((0, c1), (1, c2)):
            for e in range(3):
                for f in range(T + 2):
                    for edge in (0, H + 1):
                        z[cv, e, :, pl.ds((f * (H + 2) + edge) * W, W)] = jnp.zeros((Kp, W), BF16)

            @pl.loop(0, 2 * H)
            def _(r):
                put(cv, r // H, lax.rem(r, H), cache[:, row(r)].astype(F32))

    def activate(cv, source, gain, keep):
        final = cv * (L + 1) + L

        @pl.loop(0, T * H)
        def _(r):
            x = source[:, row(r)].astype(F32)
            scale = lax.rsqrt(sq[final, pl.ds(r, 1), :] / C + 1e-06)
            v = x * scale * gain[...]
            y = v / (1.0 + jnp.exp(-v))
            put(cv, 2 + r // H, lax.rem(r, H), y)

            @pl.when(r >= (T - 2) * H)
            def _():
                keep[:, row(r - (T - 2) * H)] = y.astype(BF16)

    def rows_at(k):
        return C >> k

    def buffer(cv, k):
        return part.at[cv] if k == 0 else summed[k - 1].at[cv]

    def copy(cv, k, c):
        if k < halvings:
            half = rows_at(k + 1)
            off = pl.multiple_of((1 - bits[k]) * half, 16)
            src = buffer(cv, k).at[c, pl.ds(off, half), :]
            dst = recv[k].at[cv, c]
        elif window:
            off = pl.multiple_of((1 - bits[k]) * (2 * Cl - Kp), 16)
            src = buffer(cv, k).at[c, pl.ds(off, Kp), :]
            dst = last_recv.at[cv, 0, c]
        else:
            j = k - halvings
            src = buffer(cv, k).at[c] if j == 0 else last_sum.at[cv, j - 1, c]
            dst = last_recv.at[cv, j, c]
        return pltpu.make_async_remote_copy(
            src_ref=src,
            dst_ref=dst,
            send_sem=send_sem.at[cv, k, c],
            recv_sem=recv_sem.at[cv, k, c],
            device_id={"chan": partner[k]},
            device_id_type=pl.DeviceIdType.MESH,
        )

    def multiply(cv, weight, c):
        t, h0 = c // nh, lax.rem(c, nh) * hc
        for a in range(3):
            for b in range(3):
                at = pl.ds(pl.multiple_of(((t + a) * (H + 2) + h0 + b) * W, W), CH)
                for e in range(3):
                    tap = 9 * a + 3 * b + e
                    xc[pl.ds(tap * Kp, Kp), :] = z[cv, e, :, at]
        part[cv, c] = jnp.dot(weight[...], xc[...], preferred_element_type=F32).astype(BF16)
        copy(cv, 0, c).start()

    def step_sum(cv, k, c, finish):
        copy(cv, k, c).wait_recv()
        if k < halvings:
            half = rows_at(k + 1)
            off = pl.multiple_of(bits[k] * half, 16)
            total = buffer(cv, k)[c, pl.ds(off, half), :].astype(F32) + recv[k][cv, c].astype(F32)
            summed[k][cv, c] = total.astype(BF16)
            copy(cv, k + 1, c).start()
            return
        if window:
            off = pl.multiple_of(bits[k] * (2 * Cl - Kp), 16)
            total = buffer(cv, k)[c, pl.ds(off, Kp), :].astype(F32) + last_recv[cv, 0, c].astype(F32)
            shift = bits[k] * (Kp - Cl)
            size = Kp
        else:
            j = k - halvings
            own = buffer(cv, k)[c] if j == 0 else last_sum[cv, j - 1, c]
            total = own.astype(F32) + last_recv[cv, j, c].astype(F32)
            if k + 1 < L:
                last_sum[cv, j, c] = total.astype(BF16)
                copy(cv, k + 1, c).start()
                return
            size = rows_at(halvings)
            shift = 0
            for i in range(rem):
                shift = shift + bits[halvings + i] * (size >> (i + 1))
        total = pltpu.roll(total, lax.rem(size - shift, size), 0)[:Kp]
        valid = lax.broadcasted_iota(jnp.int32, (Kp, CH), 0) < Cl
        finish(c, jnp.where(valid, total, 0.0))

    def convolve(cv, weight, finish):
        @pl.loop(0, nch + L)
        def _(s):
            @pl.when(s < nch)
            def _():
                multiply(cv, weight, s)

            for k in range(L - 1, -1, -1):
                c = s - 1 - k

                @pl.when(jnp.logical_and(c >= 0, c < nch))
                def _():
                    step_sum(cv, k, c, finish)

        @pl.loop(0, nch)
        def _(c):
            for k in range(L):
                copy(cv, k, c).wait_send()

    reduce_squares(0, caches)
    activate(0, feat, g1, n1)

    def finish_one(c, total):
        m = (total + b1[...]).astype(BF16)
        mid[:, pl.ds(pl.multiple_of(c * CH, W), CH)] = m
        x = m.astype(F32)
        squares = jnp.sum(x * x, axis=0, keepdims=True)
        for h in range(hc):
            sq[L + 1, pl.ds(c * hc + h, 1), :] = squares[:, h * W : (h + 1) * W]

    convolve(0, w1, finish_one)
    reduce_squares(1, lambda: None)
    activate(1, mid, g2, n2)

    def finish_two(c, total):
        at = pl.ds(pl.multiple_of(c * CH, W), CH)
        out[:, at] = (feat[:, at].astype(F32) + total + b2[...]).astype(BF16)

    convolve(1, w2, finish_two)


def shards(
    features, cache_one, cache_two, weight_one, bias_one, gain_one, weight_two, bias_two, gain_two
):
    n = lax.axis_size("chan")
    Cl, T, H, W = features.shape
    C = Cl * n
    L = n.bit_length() - 1
    Kp = -(-Cl // 16) * 16
    halvings = 0
    while halvings < L and (C >> (halvings + 1)) % 16 == 0:
        halvings += 1
    rem = L - halvings
    window = rem == 1 and (2 * Cl - Kp) % 16 == 0
    hc = H // 2 if H % 2 == 0 else H
    nh = H // hc
    nch = T * nh
    CH = hc * W
    d = dict(
        n=n, L=L, C=C, Cl=Cl, Kp=Kp, T=T, H=H, W=W, hc=hc, nh=nh, nch=nch, CH=CH,
        halvings=halvings, rem=rem, window=window,
    )

    def rows(x):
        return jnp.pad(x.reshape(Cl, -1), ((0, Kp - Cl), (0, 0)))

    def column(x):
        return jnp.pad(x, (0, Kp - Cl)).reshape(Kp, 1)

    def taps(weight):
        x = weight.reshape((Cl,) + (2,) * L + (Cl, 27))
        order = (L + 2, 0) + tuple(range(L, 0, -1)) + (L + 1,)
        x = x.transpose(order).reshape(27, Cl, C)
        return jnp.pad(x, ((0, 0), (0, Kp - Cl), (0, 0))).reshape(27 * Kp, C).T

    last_rows = Kp if window else C >> halvings
    vmem = pl.BlockSpec(memory_space=pltpu.VMEM)
    M = T * H * W
    result = pl.pallas_call(
        functools.partial(kernel, d),
        out_shape=(
            jax.ShapeDtypeStruct((Kp, M), BF16),
            jax.ShapeDtypeStruct((Kp, 2 * H * W), BF16),
            jax.ShapeDtypeStruct((Kp, 2 * H * W), BF16),
        ),
        in_specs=[vmem] * 9,
        out_specs=(vmem, vmem, vmem),
        scratch_shapes=[
            pltpu.VMEM((2, 3, Kp, (T + 2) * (H + 2) * W), BF16),
            pltpu.VMEM((27 * Kp, CH), BF16),
            pltpu.VMEM((2, nch, C, CH), BF16),
            [pltpu.VMEM((2, nch, C >> (k + 1), CH), BF16) for k in range(halvings)],
            [pltpu.VMEM((2, nch, C >> (k + 1), CH), BF16) for k in range(halvings)],
            pltpu.VMEM((2, rem, nch, last_rows, CH), BF16),
            pltpu.VMEM((2, max(rem - 1, 1), nch, last_rows if rem > 1 else 16, CH), BF16),
            pltpu.VMEM((Kp, M), BF16),
            pltpu.VMEM((2 * (L + 1), T * H, W), F32),
            pltpu.VMEM((2 * L, T * H, W), F32),
            pltpu.SemaphoreType.DMA((2, L, nch)),
            pltpu.SemaphoreType.DMA((2, L, nch)),
            pltpu.SemaphoreType.DMA((2 * L,)),
            pltpu.SemaphoreType.DMA((2 * L,)),
        ],
        compiler_params=pltpu.CompilerParams(
            collective_id=0, has_side_effects=True, vmem_limit_bytes=62 << 20
        ),
        name="resblock",
    )(
        rows(features), rows(cache_one), rows(cache_two), taps(weight_one), taps(weight_two),
        column(bias_one), column(gain_one), column(bias_two), column(gain_two),
    )
    out, one, two = result
    return (
        out[:Cl].reshape(Cl, T, H, W),
        one[:Cl].reshape(Cl, 2, H, W),
        two[:Cl].reshape(Cl, 2, H, W),
    )


def solution(mesh):
    field = P("chan", "group", None, None)
    in_specs = (
        field, field, field, P("chan", None), P("chan"), P("chan"), P("chan", None), P("chan"), P("chan"),
    )
    return jax.shard_map(
        shards, mesh=mesh, in_specs=in_specs, out_specs=(field, field, field), check_vma=False
    )
```

```python
import functools

import jax
import jax.numpy as jnp
from jax import lax
from jax.experimental import pallas as pl
from jax.experimental.pallas import tpu as pltpu
from jax.sharding import PartitionSpec as P

F32 = jnp.float32
BF16 = jnp.bfloat16


def kernel(
    d, feat, c1, c2, w1, w2, cols, out, n1, n2,
    z, wt, tmp, wq, xc, part, recv, summed, last_recv, last_sum, mid, sq, sq_recv, send_sem, recv_sem, sq_send, sq_sem,
):
    n, L, C, Cl, Kp, T, H, W = d["n"], d["L"], d["C"], d["Cl"], d["Kp"], d["T"], d["H"], d["W"]
    hc, nh, nch, CH, halvings, rem, window = (
        d["hc"], d["nh"], d["nch"], d["CH"], d["halvings"], d["rem"], d["window"]
    )
    me = lax.axis_index("chan")
    bits = [lax.rem(me // (1 << k), 2) for k in range(L)]
    partner = [me + (1 << k) * (1 - 2 * bits[k]) for k in range(L)]

    barrier = pltpu.get_barrier_semaphore()
    for k in range(L):
        pl.semaphore_signal(
            barrier, inc=1, device_id={"chan": partner[k]}, device_id_type=pl.DeviceIdType.MESH
        )

    lane = lax.broadcasted_iota(jnp.int32, (Cl, W), 1)
    per = 128 // Kp
    KW = -(-27 // per) * 128
    group = 1
    while group * Cl % 16:
        group *= 2
    b1, g1, b2, g2 = [cols.at[:, i : i + 1] for i in range(4)]
    blocks = 27 * C // 128

    def turn(w, c):
        x = w[:, pl.ds(pl.multiple_of(c * 128, 128), 128)].astype(F32)
        if x.shape[0] < Kp:
            x = jnp.concatenate([x, jnp.zeros((Kp - x.shape[0], 128), F32)], axis=0)
        wt[pl.ds(pl.multiple_of(c * 128, 128), 128), :] = jnp.concatenate([x] * per, axis=0).T

    slot = lax.broadcasted_iota(jnp.int32, (Cl, 128), 1) // Kp

    def collect(cv, j):
        for b in range(group):
            block = j * group + b
            owner = 0
            for k in range(L):
                owner = owner + lax.rem(block // (1 << (L - 1 - k)), 2) * (1 << k)
            for g in range(KW // 128):
                x = jnp.zeros((Cl, 128), F32)
                for q in range(per):
                    tap = g * per + q
                    if tap < 27:
                        x = jnp.where(slot == q, wt[pl.ds(owner * (Cl * 27) + tap, Cl, stride=27), :], x)
                tmp[b * Cl : (b + 1) * Cl, g * 128 : (g + 1) * 128] = x
        size = group * Cl
        wq[cv, pl.ds(pl.multiple_of(j * size, 16), size), :] = tmp[...].astype(BF16)

    def clear():
        for cv in range(2):
            for e in range(3):
                z[cv, e, Kp - 16 :, :] = jnp.zeros((16, (T + 2) * (H + 2) * W), BF16)
                for f in range(T + 2):
                    for edge in (0, H + 1):
                        at = (f * (H + 2) + edge) * W
                        z[cv, e, :, at : at + W] = jnp.zeros((Kp, W), BF16)
        if KW > 27 * Kp:
            xc[27 * Kp :, :] = jnp.zeros((KW - 27 * Kp, CH), BF16)

    def put(cv, frame, h, x):
        at = pl.ds(pl.multiple_of((frame * (H + 2) + h + 1) * W, W), W)
        z[cv, 1, :Cl, at] = x.astype(BF16)
        z[cv, 0, :Cl, at] = jnp.where(lane == 0, 0.0, pltpu.roll(x, 1, 1)).astype(BF16)
        z[cv, 2, :Cl, at] = jnp.where(lane == W - 1, 0.0, pltpu.roll(x, W - 1, 1)).astype(BF16)

    def row(r):
        return pl.ds(pl.multiple_of(r * W, W), W)

    @pl.loop(0, nch)
    def _(c):
        for i in range(hc):
            r = c * hc + i
            x = feat[:, row(r)].astype(F32)
            sq[0, pl.ds(r, 1), :] = jnp.sum(x * x, axis=0, keepdims=True)

    pl.semaphore_wait(barrier, L)

    def sq_copy(cv, k):
        return pltpu.make_async_remote_copy(
            src_ref=sq.at[cv * (L + 1) + k],
            dst_ref=sq_recv.at[cv * L + k],
            send_sem=sq_send.at[cv * L + k],
            recv_sem=sq_sem.at[cv * L + k],
            device_id={"chan": partner[k]},
            device_id_type=pl.DeviceIdType.MESH,
        )

    def reduce_squares(cv, work):
        sq_copy(cv, 0).start()
        for k in range(L):
            work(k)
            sq_copy(cv, k).wait_recv()
            sq[cv * (L + 1) + k + 1] = sq[cv * (L + 1) + k] + sq_recv[cv * L + k]
            if k + 1 < L:
                sq_copy(cv, k + 1).start()
        for k in range(L):
            sq_copy(cv, k).wait_send()

    def caches(cv, cache):
        @pl.loop(0, 2 * nh)
        def _(c):
            for i in range(hc):
                r = c * hc + i
                put(cv, c // nh, lax.rem(c, nh) * hc + i, cache[:, row(r)].astype(F32))

    def activate(cv, source, gain, keep):
        final = cv * (L + 1) + L

        def some(c, kept):
            for i in range(hc):
                r = c * hc + i
                x = source[:, row(r)].astype(F32)
                scale = lax.rsqrt(sq[final, pl.ds(r, 1), :] / C + 1e-06)
                v = x * scale * gain[...]
                y = v / (1.0 + jnp.exp(-v))
                put(cv, 2 + c // nh, lax.rem(c, nh) * hc + i, y)
                if kept:
                    keep[:, row(r - (T - 2) * H)] = y.astype(BF16)

        pl.loop(0, (T - 2) * nh)(lambda c: some(c, False))
        pl.loop((T - 2) * nh, nch)(lambda c: some(c, True))

    def rows_at(k):
        return C >> k

    def buffer(cv, k):
        return part.at[cv] if k == 0 else summed[k - 1].at[cv]

    def copy(cv, k, c):
        if k < halvings:
            half = rows_at(k + 1)
            off = pl.multiple_of((1 - bits[k]) * half, 16)
            src = buffer(cv, k).at[c, pl.ds(off, half), :]
            dst = recv[k].at[cv, c]
        elif window:
            off = pl.multiple_of((1 - bits[k]) * (2 * Cl - Kp), 16)
            src = buffer(cv, k).at[c, pl.ds(off, Kp), :]
            dst = last_recv.at[cv, 0, c]
        else:
            j = k - halvings
            src = buffer(cv, k).at[c] if j == 0 else last_sum.at[cv, j - 1, c]
            dst = last_recv.at[cv, j, c]
        return pltpu.make_async_remote_copy(
            src_ref=src,
            dst_ref=dst,
            send_sem=send_sem.at[cv, k, c],
            recv_sem=recv_sem.at[cv, k, c],
            device_id={"chan": partner[k]},
            device_id_type=pl.DeviceIdType.MESH,
        )

    def multiply(cv, c):
        t, h0 = c // nh, lax.rem(c, nh) * hc
        for a in range(3):
            for b in range(3):
                at = pl.ds(pl.multiple_of(((t + a) * (H + 2) + h0 + b) * W, W), CH)
                for e in range(3):
                    tap = 9 * a + 3 * b + e
                    xc[pl.ds(tap * Kp, Kp), :] = z[cv, e, :, at]
        part[cv, c] = jnp.dot(wq[cv], xc[...], preferred_element_type=F32).astype(BF16)
        copy(cv, 0, c).start()

    def step_sum(cv, k, c, finish):
        copy(cv, k, c).wait_recv()
        if k < halvings:
            half = rows_at(k + 1)
            off = pl.multiple_of(bits[k] * half, 16)
            total = buffer(cv, k)[c, pl.ds(off, half), :].astype(F32) + recv[k][cv, c].astype(F32)
            summed[k][cv, c] = total.astype(BF16)
            copy(cv, k + 1, c).start()
            return
        if window:
            off = pl.multiple_of(bits[k] * (2 * Cl - Kp), 16)
            total = buffer(cv, k)[c, pl.ds(off, Kp), :].astype(F32) + last_recv[cv, 0, c].astype(F32)
            shift = bits[k] * (Kp - Cl)
            size = Kp
        else:
            j = k - halvings
            own = buffer(cv, k)[c] if j == 0 else last_sum[cv, j - 1, c]
            total = own.astype(F32) + last_recv[cv, j, c].astype(F32)
            if k + 1 < L:
                last_sum[cv, j, c] = total.astype(BF16)
                copy(cv, k + 1, c).start()
                return
            size = rows_at(halvings)
            shift = 0
            for i in range(rem):
                shift = shift + bits[halvings + i] * (size >> (i + 1))
        total = pltpu.roll(total, lax.rem(size - shift, size), 0)[:Cl]
        finish(c, total)

    def convolve(cv, finish, work):
        @pl.loop(0, nch + L)
        def _(s):
            @pl.when(s < nch)
            def _():
                multiply(cv, s)

            work(s)

            for k in range(L - 1, -1, -1):
                c = s - 1 - k

                @pl.when(jnp.logical_and(c >= 0, c < nch))
                def _():
                    step_sum(cv, k, c, finish)

        @pl.loop(0, nch)
        def _(c):
            for k in range(L):
                copy(cv, k, c).wait_send()

    groups = n // group

    def first_work(k):
        if k == 0:
            @pl.loop(0, blocks // 3)
            def _(c):
                for i in range(3):
                    turn(w1, c * 3 + i)
        if k == min(1, L - 1):
            clear()
            caches(0, c1)
        if k == L - 1:
            pl.loop(0, groups)(lambda j: collect(0, j))

    reduce_squares(0, first_work)
    activate(0, feat, g1, n1)

    turns = -(-blocks // (nch + L))

    def turn_two(s):
        for i in range(turns):
            turn(w2, jnp.minimum(s * turns + i, blocks - 1))

    def finish_one(c, total):
        m = (total + b1[...]).astype(BF16)
        mid[:, pl.ds(pl.multiple_of(c * CH, W), CH)] = m
        x = m.astype(F32)
        squares = jnp.sum(x * x, axis=0, keepdims=True)
        for h in range(hc):
            sq[L + 1, pl.ds(c * hc + h, 1), :] = squares[:, h * W : (h + 1) * W]

    convolve(0, finish_one, turn_two)

    def second_work(k):
        if k == 0:
            caches(1, c2)
        first, stop = k * groups // L, (k + 1) * groups // L
        pl.loop(first, stop)(lambda j: collect(1, j))

    reduce_squares(1, second_work)
    activate(1, mid, g2, n2)

    def finish_two(c, total):
        at = pl.ds(pl.multiple_of(c * CH, W), CH)
        out[:, at] = (feat[:, at].astype(F32) + total + b2[...]).astype(BF16)

    convolve(1, finish_two, lambda s: None)


def shards(
    features, cache_one, cache_two, weight_one, bias_one, gain_one, weight_two, bias_two, gain_two
):
    n = lax.axis_size("chan")
    Cl, T, H, W = features.shape
    C = Cl * n
    L = n.bit_length() - 1
    Kp = -(-Cl // 16) * 16
    halvings = 0
    while halvings < L and (C >> (halvings + 1)) % 16 == 0:
        halvings += 1
    rem = L - halvings
    window = rem == 1 and (2 * Cl - Kp) % 16 == 0
    hc = H // 2 if H % 2 == 0 else H
    nh = H // hc
    nch = T * nh
    CH = hc * W
    d = dict(
        n=n, L=L, C=C, Cl=Cl, Kp=Kp, T=T, H=H, W=W, hc=hc, nh=nh, nch=nch, CH=CH,
        halvings=halvings, rem=rem, window=window,
    )

    def rows(x):
        return x.reshape(Cl, -1)

    def taps(weight):
        return weight if Cl % 8 == 0 else jnp.pad(weight, ((0, Kp - Cl), (0, 0)))

    per = 128 // Kp
    KW = -(-27 // per) * 128
    group = 1
    while group * Cl % 16:
        group *= 2
    last_rows = Kp if window else C >> halvings
    vmem = pl.BlockSpec(memory_space=pltpu.VMEM)
    M = T * H * W
    result = pl.pallas_call(
        functools.partial(kernel, d),
        out_shape=(
            jax.ShapeDtypeStruct((Cl, M), BF16),
            jax.ShapeDtypeStruct((Cl, 2 * H * W), BF16),
            jax.ShapeDtypeStruct((Cl, 2 * H * W), BF16),
        ),
        in_specs=[vmem] * 6,
        out_specs=(vmem, vmem, vmem),
        scratch_shapes=[
            pltpu.VMEM((2, 3, Kp, (T + 2) * (H + 2) * W), BF16),
            pltpu.VMEM((27 * C, 128), F32),
            pltpu.VMEM((group * Cl, KW), F32),
            pltpu.VMEM((2, C, KW), BF16),
            pltpu.VMEM((KW, CH), BF16),
            pltpu.VMEM((2, nch, C, CH), BF16),
            [pltpu.VMEM((2, nch, C >> (k + 1), CH), BF16) for k in range(halvings)],
            [pltpu.VMEM((2, nch, C >> (k + 1), CH), BF16) for k in range(halvings)],
            pltpu.VMEM((2, rem, nch, last_rows, CH), BF16),
            pltpu.VMEM((2, max(rem - 1, 1), nch, last_rows if rem > 1 else 16, CH), BF16),
            pltpu.VMEM((Cl, M), BF16),
            pltpu.VMEM((2 * (L + 1), T * H, W), F32),
            pltpu.VMEM((2 * L, T * H, W), F32),
            pltpu.SemaphoreType.DMA((2, L, nch)),
            pltpu.SemaphoreType.DMA((2, L, nch)),
            pltpu.SemaphoreType.DMA((2 * L,)),
            pltpu.SemaphoreType.DMA((2 * L,)),
        ],
        compiler_params=pltpu.CompilerParams(
            collective_id=0, has_side_effects=True, vmem_limit_bytes=62 << 20
        ),
        name="resblock",
    )(
        rows(features), rows(cache_one), rows(cache_two), taps(weight_one), taps(weight_two),
        jnp.stack((bias_one, gain_one, bias_two, gain_two), axis=1),
    )
    out, one, two = result
    return (
        out.reshape(Cl, T, H, W),
        one.reshape(Cl, 2, H, W),
        two.reshape(Cl, 2, H, W),
    )


def solution(mesh):
    field = P("chan", "group", None, None)
    in_specs = (
        field, field, field, P("chan", None), P("chan"), P("chan"), P("chan", None), P("chan"), P("chan"),
    )
    return jax.shard_map(
        shards, mesh=mesh, in_specs=in_specs, out_specs=(field, field, field), check_vma=False
    )
```

```python
import functools

import jax
import jax.numpy as jnp
from jax import lax
from jax.experimental import pallas as pl
from jax.experimental.pallas import tpu as pltpu
from jax.sharding import PartitionSpec as P

F32 = jnp.float32
BF16 = jnp.bfloat16
CHUNK_ROWS = 6
FIRST_LAG = 1
LAG = 2


def kernel(
    d, feat, c1, c2, w1, w2, cols, out, n1, n2,
    z, wt, tmp, wq, xc, part, recv, summed, last_recv, last_sum, mid, sq, sq_recv, send_sem, recv_sem, sq_send, sq_sem,
):
    n, L, C, Cl, Kp, T, H, W = d["n"], d["L"], d["C"], d["Cl"], d["Kp"], d["T"], d["H"], d["W"]
    hc, nh, nch, CH, halvings, rem, window = (
        d["hc"], d["nh"], d["nch"], d["CH"], d["halvings"], d["rem"], d["window"]
    )
    lags = d["lags"]
    me = lax.axis_index("chan")
    bits = [lax.rem(me // (1 << k), 2) for k in range(L)]
    partner = [me + (1 << k) * (1 - 2 * bits[k]) for k in range(L)]

    barrier = pltpu.get_barrier_semaphore()
    for k in range(L):
        pl.semaphore_signal(
            barrier, inc=1, device_id={"chan": partner[k]}, device_id_type=pl.DeviceIdType.MESH
        )

    lane = lax.broadcasted_iota(jnp.int32, (Cl, W), 1)
    per = 128 // Kp
    KW = -(-27 // per) * 128
    group = 1
    while group * Cl % 16:
        group *= 2
    b1, g1, b2, g2 = [cols.at[:, i : i + 1] for i in range(4)]
    blocks = 27 * C // 128

    def turn(w, c):
        x = w[:, pl.ds(pl.multiple_of(c * 128, 128), 128)].astype(F32)
        if x.shape[0] < Kp:
            x = jnp.concatenate([x, jnp.zeros((Kp - x.shape[0], 128), F32)], axis=0)
        wt[pl.ds(pl.multiple_of(c * 128, 128), 128), :] = jnp.concatenate([x] * per, axis=0).T

    slot = lax.broadcasted_iota(jnp.int32, (Cl, 128), 1) // Kp

    def collect(cv, j):
        for b in range(group):
            block = j * group + b
            owner = 0
            for k in range(L):
                owner = owner + lax.rem(block // (1 << (L - 1 - k)), 2) * (1 << k)
            for g in range(KW // 128):
                x = jnp.zeros((Cl, 128), F32)
                for q in range(per):
                    tap = g * per + q
                    if tap < 27:
                        x = jnp.where(slot == q, wt[pl.ds(owner * (Cl * 27) + tap, Cl, stride=27), :], x)
                tmp[b * Cl : (b + 1) * Cl, g * 128 : (g + 1) * 128] = x
        size = group * Cl
        wq[cv, pl.ds(pl.multiple_of(j * size, 16), size), :] = tmp[...].astype(BF16)

    def clear():
        for cv in range(2):
            for e in range(3):
                z[cv, e, Kp - 16 :, :] = jnp.zeros((16, (T + 2) * (H + 2) * W), BF16)
                for f in range(T + 2):
                    for edge in (0, H + 1):
                        at = (f * (H + 2) + edge) * W
                        z[cv, e, :, at : at + W] = jnp.zeros((Kp, W), BF16)
        if KW > 27 * Kp:
            xc[27 * Kp :, :] = jnp.zeros((KW - 27 * Kp, CH), BF16)

    def put(cv, frame, h, x):
        at = pl.ds(pl.multiple_of((frame * (H + 2) + h + 1) * W, W), W)
        z[cv, 1, :Cl, at] = x.astype(BF16)
        z[cv, 0, :Cl, at] = jnp.where(lane == 0, 0.0, pltpu.roll(x, 1, 1)).astype(BF16)
        z[cv, 2, :Cl, at] = jnp.where(lane == W - 1, 0.0, pltpu.roll(x, W - 1, 1)).astype(BF16)

    def row(r):
        return pl.ds(pl.multiple_of(r * W, W), W)

    @pl.loop(0, nch)
    def _(c):
        for i in range(hc):
            r = c * hc + i
            x = feat[:, row(r)].astype(F32)
            sq[0, pl.ds(r, 1), :] = jnp.sum(x * x, axis=0, keepdims=True)

    pl.semaphore_wait(barrier, L)

    def sq_copy(cv, k):
        return pltpu.make_async_remote_copy(
            src_ref=sq.at[cv * (L + 1) + k],
            dst_ref=sq_recv.at[cv * L + k],
            send_sem=sq_send.at[cv * L + k],
            recv_sem=sq_sem.at[cv * L + k],
            device_id={"chan": partner[k]},
            device_id_type=pl.DeviceIdType.MESH,
        )

    def reduce_squares(cv, work):
        sq_copy(cv, 0).start()
        for k in range(L):
            work(k)
            sq_copy(cv, k).wait_recv()
            sq[cv * (L + 1) + k + 1] = sq[cv * (L + 1) + k] + sq_recv[cv * L + k]
            if k + 1 < L:
                sq_copy(cv, k + 1).start()
        for k in range(L):
            sq_copy(cv, k).wait_send()

    def caches(cv, cache):
        @pl.loop(0, 2 * nh)
        def _(c):
            for i in range(hc):
                r = c * hc + i
                put(cv, c // nh, lax.rem(c, nh) * hc + i, cache[:, row(r)].astype(F32))

    def activate(cv, source, gain, keep):
        final = cv * (L + 1) + L

        def some(c, kept):
            for i in range(hc):
                r = c * hc + i
                x = source[:, row(r)].astype(F32)
                scale = lax.rsqrt(sq[final, pl.ds(r, 1), :] / C + 1e-06)
                v = x * scale * gain[...]
                y = v / (1.0 + jnp.exp(-v))
                put(cv, 2 + c // nh, lax.rem(c, nh) * hc + i, y)
                if kept:
                    keep[:, row(r - (T - 2) * H)] = y.astype(BF16)

        pl.loop(0, (T - 2) * nh)(lambda c: some(c, False))
        pl.loop((T - 2) * nh, nch)(lambda c: some(c, True))

    def rows_at(k):
        return C >> k

    def buffer(cv, k):
        return part.at[cv] if k == 0 else summed[k - 1].at[cv]

    def copy(cv, k, c):
        if k < halvings:
            half = rows_at(k + 1)
            off = pl.multiple_of((1 - bits[k]) * half, 16)
            src = buffer(cv, k).at[c, pl.ds(off, half), :]
            dst = recv[k].at[cv, c]
        elif window:
            off = pl.multiple_of((1 - bits[k]) * (2 * Cl - Kp), 16)
            src = buffer(cv, k).at[c, pl.ds(off, Kp), :]
            dst = last_recv.at[cv, 0, c]
        else:
            j = k - halvings
            src = buffer(cv, k).at[c] if j == 0 else last_sum.at[cv, j - 1, c]
            dst = last_recv.at[cv, j, c]
        return pltpu.make_async_remote_copy(
            src_ref=src,
            dst_ref=dst,
            send_sem=send_sem.at[cv, k, c],
            recv_sem=recv_sem.at[cv, k, c],
            device_id={"chan": partner[k]},
            device_id_type=pl.DeviceIdType.MESH,
        )

    def multiply(cv, c):
        t, h0 = c // nh, lax.rem(c, nh) * hc
        for a in range(3):
            for b in range(3):
                at = pl.ds(pl.multiple_of(((t + a) * (H + 2) + h0 + b) * W, W), CH)
                for e in range(3):
                    tap = 9 * a + 3 * b + e
                    xc[pl.ds(tap * Kp, Kp), :] = z[cv, e, :, at]
        part[cv, c] = jnp.dot(wq[cv], xc[...], preferred_element_type=F32).astype(BF16)
        copy(cv, 0, c).start()

    def step_sum(cv, k, c, finish):
        copy(cv, k, c).wait_recv()
        if k < halvings:
            half = rows_at(k + 1)
            off = pl.multiple_of(bits[k] * half, 16)
            total = buffer(cv, k)[c, pl.ds(off, half), :].astype(F32) + recv[k][cv, c].astype(F32)
            summed[k][cv, c] = total.astype(BF16)
            copy(cv, k + 1, c).start()
            return
        if window:
            off = pl.multiple_of(bits[k] * (2 * Cl - Kp), 16)
            total = buffer(cv, k)[c, pl.ds(off, Kp), :].astype(F32) + last_recv[cv, 0, c].astype(F32)
            shift = bits[k] * (Kp - Cl)
            size = Kp
        else:
            j = k - halvings
            own = buffer(cv, k)[c] if j == 0 else last_sum[cv, j - 1, c]
            total = own.astype(F32) + last_recv[cv, j, c].astype(F32)
            if k + 1 < L:
                last_sum[cv, j, c] = total.astype(BF16)
                copy(cv, k + 1, c).start()
                return
            size = rows_at(halvings)
            shift = 0
            for i in range(rem):
                shift = shift + bits[halvings + i] * (size >> (i + 1))
        total = pltpu.roll(total, lax.rem(size - shift, size), 0)[:Cl]
        finish(c, total)

    def convolve(cv, finish, work):
        @pl.loop(0, nch + lags[-1])
        def _(s):
            @pl.when(s < nch)
            def _():
                multiply(cv, s)

            work(s)

            for k in range(L - 1, -1, -1):
                c = s - lags[k]

                @pl.when(jnp.logical_and(c >= 0, c < nch))
                def _():
                    step_sum(cv, k, c, finish)

        @pl.loop(0, nch)
        def _(c):
            for k in range(L):
                copy(cv, k, c).wait_send()

    groups = n // group

    def first_work(k):
        if k == 0:
            @pl.loop(0, blocks // 3)
            def _(c):
                for i in range(3):
                    turn(w1, c * 3 + i)
        if k == min(1, L - 1):
            clear()
            caches(0, c1)
        if k == L - 1:
            pl.loop(0, groups)(lambda j: collect(0, j))

    reduce_squares(0, first_work)
    activate(0, feat, g1, n1)

    turns = -(-blocks // (nch + lags[-1]))

    def turn_two(s):
        for i in range(turns):
            turn(w2, jnp.minimum(s * turns + i, blocks - 1))

    def finish_one(c, total):
        m = (total + b1[...]).astype(BF16)
        mid[:, pl.ds(pl.multiple_of(c * CH, W), CH)] = m
        x = m.astype(F32)
        squares = jnp.sum(x * x, axis=0, keepdims=True)
        for h in range(hc):
            sq[L + 1, pl.ds(c * hc + h, 1), :] = squares[:, h * W : (h + 1) * W]

    convolve(0, finish_one, turn_two)

    def second_work(k):
        if k == 0:
            caches(1, c2)
        first, stop = k * groups // L, (k + 1) * groups // L
        pl.loop(first, stop)(lambda j: collect(1, j))

    reduce_squares(1, second_work)
    activate(1, mid, g2, n2)

    def finish_two(c, total):
        at = pl.ds(pl.multiple_of(c * CH, W), CH)
        out[:, at] = (feat[:, at].astype(F32) + total + b2[...]).astype(BF16)

    convolve(1, finish_two, lambda s: None)


def shards(
    features, cache_one, cache_two, weight_one, bias_one, gain_one, weight_two, bias_two, gain_two
):
    n = lax.axis_size("chan")
    Cl, T, H, W = features.shape
    C = Cl * n
    L = n.bit_length() - 1
    Kp = -(-Cl // 16) * 16
    halvings = 0
    while halvings < L and (C >> (halvings + 1)) % 16 == 0:
        halvings += 1
    rem = L - halvings
    window = rem == 1 and (2 * Cl - Kp) % 16 == 0
    hc = max(h for h in range(1, CHUNK_ROWS + 1) if H % h == 0)
    lags = [FIRST_LAG + LAG * k for k in range(L)]
    nh = H // hc
    nch = T * nh
    CH = hc * W
    d = dict(
        n=n, L=L, C=C, Cl=Cl, Kp=Kp, T=T, H=H, W=W, hc=hc, nh=nh, nch=nch, CH=CH,
        halvings=halvings, rem=rem, window=window, lags=lags,
    )

    def rows(x):
        return x.reshape(Cl, -1)

    def taps(weight):
        return weight if Cl % 8 == 0 else jnp.pad(weight, ((0, Kp - Cl), (0, 0)))

    per = 128 // Kp
    KW = -(-27 // per) * 128
    group = 1
    while group * Cl % 16:
        group *= 2
    last_rows = Kp if window else C >> halvings
    vmem = pl.BlockSpec(memory_space=pltpu.VMEM)
    M = T * H * W
    result = pl.pallas_call(
        functools.partial(kernel, d),
        out_shape=(
            jax.ShapeDtypeStruct((Cl, M), BF16),
            jax.ShapeDtypeStruct((Cl, 2 * H * W), BF16),
            jax.ShapeDtypeStruct((Cl, 2 * H * W), BF16),
        ),
        in_specs=[vmem] * 6,
        out_specs=(vmem, vmem, vmem),
        scratch_shapes=[
            pltpu.VMEM((2, 3, Kp, (T + 2) * (H + 2) * W), BF16),
            pltpu.VMEM((27 * C, 128), F32),
            pltpu.VMEM((group * Cl, KW), F32),
            pltpu.VMEM((2, C, KW), BF16),
            pltpu.VMEM((KW, CH), BF16),
            pltpu.VMEM((2, nch, C, CH), BF16),
            [pltpu.VMEM((2, nch, C >> (k + 1), CH), BF16) for k in range(halvings)],
            [pltpu.VMEM((2, nch, C >> (k + 1), CH), BF16) for k in range(halvings)],
            pltpu.VMEM((2, rem, nch, last_rows, CH), BF16),
            pltpu.VMEM((2, max(rem - 1, 1), nch, last_rows if rem > 1 else 16, CH), BF16),
            pltpu.VMEM((Cl, M), BF16),
            pltpu.VMEM((2 * (L + 1), T * H, W), F32),
            pltpu.VMEM((2 * L, T * H, W), F32),
            pltpu.SemaphoreType.DMA((2, L, nch)),
            pltpu.SemaphoreType.DMA((2, L, nch)),
            pltpu.SemaphoreType.DMA((2 * L,)),
            pltpu.SemaphoreType.DMA((2 * L,)),
        ],
        compiler_params=pltpu.CompilerParams(
            collective_id=0, has_side_effects=True, vmem_limit_bytes=62 << 20
        ),
        name="resblock",
    )(
        rows(features), rows(cache_one), rows(cache_two), taps(weight_one), taps(weight_two),
        jnp.stack((bias_one, gain_one, bias_two, gain_two), axis=1),
    )
    out, one, two = result
    return (
        out.reshape(Cl, T, H, W),
        one.reshape(Cl, 2, H, W),
        two.reshape(Cl, 2, H, W),
    )


def solution(mesh):
    field = P("chan", "group", None, None)
    in_specs = (
        field, field, field, P("chan", None), P("chan"), P("chan"), P("chan", None), P("chan"), P("chan"),
    )
    return jax.shard_map(
        shards, mesh=mesh, in_specs=in_specs, out_specs=(field, field, field), check_vma=False
    )
```

```python
import functools

import jax
import jax.numpy as jnp
from jax import lax
from jax.experimental import pallas as pl
from jax.experimental.pallas import tpu as pltpu
from jax.sharding import PartitionSpec as P

F32 = jnp.float32
BF16 = jnp.bfloat16
CHUNK_ROWS = 6
FIRST_LAG = 1
LAG = 2


def kernel(
    d, feat, c1, c2, w1, w2, cols, out, n1, n2,
    z, wt, tmp, wq, xc, part, recv, summed, last_recv, last_sum, mid, sq, sq_recv, send_sem, recv_sem, sq_send, sq_sem,
):
    n, L, C, Cl, Kp, T, H, W = d["n"], d["L"], d["C"], d["Cl"], d["Kp"], d["T"], d["H"], d["W"]
    hc, nh, nch, CH, halvings, rem, window = (
        d["hc"], d["nh"], d["nch"], d["CH"], d["halvings"], d["rem"], d["window"]
    )
    lags = d["lags"]
    me = lax.axis_index("chan")
    bits = [lax.rem(me // (1 << k), 2) for k in range(L)]
    partner = [me + (1 << k) * (1 - 2 * bits[k]) for k in range(L)]

    barrier = pltpu.get_barrier_semaphore()
    for k in range(L):
        pl.semaphore_signal(
            barrier, inc=1, device_id={"chan": partner[k]}, device_id_type=pl.DeviceIdType.MESH
        )

    lane = lax.broadcasted_iota(jnp.int32, (Cl, W), 1)
    per = 128 // Kp
    KW = -(-27 // per) * 128
    group = 1
    while group * Cl % 16:
        group *= 2
    b1, g1, b2, g2 = [cols.at[:, i : i + 1] for i in range(4)]
    blocks = 27 * C // 128

    def turn(w, c):
        x = w[:, pl.ds(pl.multiple_of(c * 128, 128), 128)].astype(F32)
        if x.shape[0] < Kp:
            x = jnp.concatenate([x, jnp.zeros((Kp - x.shape[0], 128), F32)], axis=0)
        wt[pl.ds(pl.multiple_of(c * 128, 128), 128), :] = jnp.concatenate([x] * per, axis=0).T

    slot = lax.broadcasted_iota(jnp.int32, (Cl, 128), 1) // Kp

    def collect(cv, j):
        for b in range(group):
            block = j * group + b
            owner = 0
            for k in range(L):
                owner = owner + lax.rem(block // (1 << (L - 1 - k)), 2) * (1 << k)
            for g in range(KW // 128):
                x = jnp.zeros((Cl, 128), F32)
                for q in range(per):
                    tap = g * per + q
                    if tap < 27:
                        x = jnp.where(slot == q, wt[pl.ds(owner * (Cl * 27) + tap, Cl, stride=27), :], x)
                tmp[b * Cl : (b + 1) * Cl, g * 128 : (g + 1) * 128] = x
        size = group * Cl
        wq[cv, pl.ds(pl.multiple_of(j * size, 16), size), :] = tmp[...].astype(BF16)

    def clear():
        for cv in range(2):
            for e in range(3):
                z[cv, e, Kp - 16 :, :] = jnp.zeros((16, (T + 2) * (H + 2) * W), BF16)
                for f in range(T + 2):
                    for edge in (0, H + 1):
                        at = (f * (H + 2) + edge) * W
                        z[cv, e, :, at : at + W] = jnp.zeros((Kp, W), BF16)
        if KW > 27 * Kp:
            xc[27 * Kp :, :] = jnp.zeros((KW - 27 * Kp, CH), BF16)

    def put(cv, frame, h, x):
        at = pl.ds(pl.multiple_of((frame * (H + 2) + h + 1) * W, W), W)
        z[cv, 1, :Cl, at] = x.astype(BF16)
        z[cv, 0, :Cl, at] = jnp.where(lane == 0, 0.0, pltpu.roll(x, 1, 1)).astype(BF16)
        z[cv, 2, :Cl, at] = jnp.where(lane == W - 1, 0.0, pltpu.roll(x, W - 1, 1)).astype(BF16)

    def row(r):
        return pl.ds(pl.multiple_of(r * W, W), W)

    @pl.loop(0, nch)
    def _(c):
        for i in range(hc):
            r = c * hc + i
            x = feat[:, row(r)].astype(F32)
            sq[0, pl.ds(r, 1), :] = jnp.sum(x * x, axis=0, keepdims=True)

    pl.semaphore_wait(barrier, L)

    def sq_copy(cv, k):
        return pltpu.make_async_remote_copy(
            src_ref=sq.at[cv * (L + 1) + k],
            dst_ref=sq_recv.at[cv * L + k],
            send_sem=sq_send.at[cv * L + k],
            recv_sem=sq_sem.at[cv * L + k],
            device_id={"chan": partner[k]},
            device_id_type=pl.DeviceIdType.MESH,
        )

    def reduce_squares(cv, work):
        sq_copy(cv, 0).start()
        for k in range(L):
            work(k)
            sq_copy(cv, k).wait_recv()
            sq[cv * (L + 1) + k + 1] = sq[cv * (L + 1) + k] + sq_recv[cv * L + k]
            if k + 1 < L:
                sq_copy(cv, k + 1).start()
        for k in range(L):
            sq_copy(cv, k).wait_send()

    def caches(cv, cache):
        @pl.loop(0, 2 * nh)
        def _(c):
            for i in range(hc):
                r = c * hc + i
                put(cv, c // nh, lax.rem(c, nh) * hc + i, cache[:, row(r)].astype(F32))

    def activate(cv, source, gain, keep):
        final = cv * (L + 1) + L

        def some(c, kept):
            for i in range(hc):
                r = c * hc + i
                x = source[:, row(r)].astype(F32)
                scale = lax.rsqrt(sq[final, pl.ds(r, 1), :] / C + 1e-06)
                v = x * scale * gain[...]
                y = v / (1.0 + jnp.exp(-v))
                put(cv, 2 + c // nh, lax.rem(c, nh) * hc + i, y)
                if kept:
                    keep[:, row(r - (T - 2) * H)] = y.astype(BF16)

        pl.loop(0, (T - 2) * nh)(lambda c: some(c, False))
        pl.loop((T - 2) * nh, nch)(lambda c: some(c, True))

    def rows_at(k):
        return C >> k

    def buffer(cv, k):
        return part.at[cv] if k == 0 else summed[k - 1].at[cv]

    def copy(cv, k, c):
        if k < halvings:
            half = rows_at(k + 1)
            off = pl.multiple_of((1 - bits[k]) * half, 16)
            src = buffer(cv, k).at[c, pl.ds(off, half), :]
            dst = recv[k].at[cv, c]
        elif window:
            off = pl.multiple_of((1 - bits[k]) * (2 * Cl - Kp), 16)
            src = buffer(cv, k).at[c, pl.ds(off, Kp), :]
            dst = last_recv.at[cv, 0, c]
        else:
            j = k - halvings
            src = buffer(cv, k).at[c] if j == 0 else last_sum.at[cv, j - 1, c]
            dst = last_recv.at[cv, j, c]
        return pltpu.make_async_remote_copy(
            src_ref=src,
            dst_ref=dst,
            send_sem=send_sem.at[cv, k, c],
            recv_sem=recv_sem.at[cv, k, c],
            device_id={"chan": partner[k]},
            device_id_type=pl.DeviceIdType.MESH,
        )

    def multiply(cv, c):
        t, h0 = c // nh, lax.rem(c, nh) * hc
        for a in range(3):
            for b in range(3):
                at = pl.ds(pl.multiple_of(((t + a) * (H + 2) + h0 + b) * W, W), CH)
                for e in range(3):
                    tap = 9 * a + 3 * b + e
                    xc[pl.ds(tap * Kp, Kp), :] = z[cv, e, :, at]
        part[cv, c] = jnp.dot(wq[cv], xc[...], preferred_element_type=F32).astype(BF16)
        copy(cv, 0, c).start()

    def step_sum(cv, k, c, finish):
        copy(cv, k, c).wait_recv()
        if k < halvings:
            half = rows_at(k + 1)
            off = pl.multiple_of(bits[k] * half, 16)
            total = buffer(cv, k)[c, pl.ds(off, half), :].astype(F32) + recv[k][cv, c].astype(F32)
            summed[k][cv, c] = total.astype(BF16)
            copy(cv, k + 1, c).start()
            return
        if window:
            off = pl.multiple_of(bits[k] * (2 * Cl - Kp), 16)
            total = buffer(cv, k)[c, pl.ds(off, Kp), :].astype(F32) + last_recv[cv, 0, c].astype(F32)
            shift = bits[k] * (Kp - Cl)
            size = Kp
        else:
            j = k - halvings
            own = buffer(cv, k)[c] if j == 0 else last_sum[cv, j - 1, c]
            total = own.astype(F32) + last_recv[cv, j, c].astype(F32)
            if k + 1 < L:
                last_sum[cv, j, c] = total.astype(BF16)
                copy(cv, k + 1, c).start()
                return
            size = rows_at(halvings)
            shift = 0
            for i in range(rem):
                shift = shift + bits[halvings + i] * (size >> (i + 1))
        total = pltpu.roll(total, lax.rem(size - shift, size), 0)[:Cl]
        finish(c, total)

    def convolve(cv, finish, work):
        @pl.loop(0, nch + lags[-1])
        def _(s):
            @pl.when(s < nch)
            def _():
                multiply(cv, s)

            work(s)

            for k in range(L - 1, -1, -1):
                c = s - lags[k]

                @pl.when(jnp.logical_and(c >= 0, c < nch))
                def _():
                    step_sum(cv, k, c, finish)

        @pl.loop(0, nch)
        def _(c):
            for k in range(L):
                copy(cv, k, c).wait_send()

    groups = n // group

    def first_work(k):
        if k == 0:
            clear()
        if k in (1, 2):
            half = blocks // 6
            lo, hi = (0, half) if k == 1 else (half, blocks // 3)

            @pl.loop(lo, hi)
            def _(c):
                for i in range(3):
                    turn(w1, c * 3 + i)
        if k == L - 1:
            caches(0, c1)
        if k == L - 1:
            pl.loop(0, groups)(lambda j: collect(0, j))

    reduce_squares(0, first_work)
    activate(0, feat, g1, n1)

    turns = -(-blocks // (nch + lags[-1]))

    def turn_two(s):
        for i in range(turns):
            turn(w2, jnp.minimum(s * turns + i, blocks - 1))

    def finish_one(c, total):
        m = (total + b1[...]).astype(BF16)
        mid[:, pl.ds(pl.multiple_of(c * CH, W), CH)] = m
        x = m.astype(F32)
        squares = jnp.sum(x * x, axis=0, keepdims=True)
        for h in range(hc):
            sq[L + 1, pl.ds(c * hc + h, 1), :] = squares[:, h * W : (h + 1) * W]

    convolve(0, finish_one, turn_two)

    def second_work(k):
        if k == 0:
            caches(1, c2)
        first, stop = k * groups // L, (k + 1) * groups // L
        pl.loop(first, stop)(lambda j: collect(1, j))

    reduce_squares(1, second_work)
    activate(1, mid, g2, n2)

    def finish_two(c, total):
        at = pl.ds(pl.multiple_of(c * CH, W), CH)
        out[:, at] = (feat[:, at].astype(F32) + total + b2[...]).astype(BF16)

    convolve(1, finish_two, lambda s: None)


def shards(
    features, cache_one, cache_two, weight_one, bias_one, gain_one, weight_two, bias_two, gain_two
):
    n = lax.axis_size("chan")
    Cl, T, H, W = features.shape
    C = Cl * n
    L = n.bit_length() - 1
    Kp = -(-Cl // 16) * 16
    halvings = 0
    while halvings < L and (C >> (halvings + 1)) % 16 == 0:
        halvings += 1
    rem = L - halvings
    window = rem == 1 and (2 * Cl - Kp) % 16 == 0
    hc = max(h for h in range(1, CHUNK_ROWS + 1) if H % h == 0)
    lags = [FIRST_LAG + LAG * k for k in range(L)]
    nh = H // hc
    nch = T * nh
    CH = hc * W
    d = dict(
        n=n, L=L, C=C, Cl=Cl, Kp=Kp, T=T, H=H, W=W, hc=hc, nh=nh, nch=nch, CH=CH,
        halvings=halvings, rem=rem, window=window, lags=lags,
    )

    def rows(x):
        return x.reshape(Cl, -1)

    def taps(weight):
        return weight if Cl % 8 == 0 else jnp.pad(weight, ((0, Kp - Cl), (0, 0)))

    per = 128 // Kp
    KW = -(-27 // per) * 128
    group = 1
    while group * Cl % 16:
        group *= 2
    last_rows = Kp if window else C >> halvings
    vmem = pl.BlockSpec(memory_space=pltpu.VMEM)
    M = T * H * W
    result = pl.pallas_call(
        functools.partial(kernel, d),
        out_shape=(
            jax.ShapeDtypeStruct((Cl, M), BF16),
            jax.ShapeDtypeStruct((Cl, 2 * H * W), BF16),
            jax.ShapeDtypeStruct((Cl, 2 * H * W), BF16),
        ),
        in_specs=[vmem] * 6,
        out_specs=(vmem, vmem, vmem),
        scratch_shapes=[
            pltpu.VMEM((2, 3, Kp, (T + 2) * (H + 2) * W), BF16),
            pltpu.VMEM((27 * C, 128), F32),
            pltpu.VMEM((group * Cl, KW), F32),
            pltpu.VMEM((2, C, KW), BF16),
            pltpu.VMEM((KW, CH), BF16),
            pltpu.VMEM((2, nch, C, CH), BF16),
            [pltpu.VMEM((2, nch, C >> (k + 1), CH), BF16) for k in range(halvings)],
            [pltpu.VMEM((2, nch, C >> (k + 1), CH), BF16) for k in range(halvings)],
            pltpu.VMEM((2, rem, nch, last_rows, CH), BF16),
            pltpu.VMEM((2, max(rem - 1, 1), nch, last_rows if rem > 1 else 16, CH), BF16),
            pltpu.VMEM((Cl, M), BF16),
            pltpu.VMEM((2 * (L + 1), T * H, W), F32),
            pltpu.VMEM((2 * L, T * H, W), F32),
            pltpu.SemaphoreType.DMA((2, L, nch)),
            pltpu.SemaphoreType.DMA((2, L, nch)),
            pltpu.SemaphoreType.DMA((2 * L,)),
            pltpu.SemaphoreType.DMA((2 * L,)),
        ],
        compiler_params=pltpu.CompilerParams(
            collective_id=0, has_side_effects=True, vmem_limit_bytes=62 << 20
        ),
        name="resblock",
    )(
        rows(features), rows(cache_one), rows(cache_two), taps(weight_one), taps(weight_two),
        jnp.stack((bias_one, gain_one, bias_two, gain_two), axis=1),
    )
    out, one, two = result
    return (
        out.reshape(Cl, T, H, W),
        one.reshape(Cl, 2, H, W),
        two.reshape(Cl, 2, H, W),
    )


def solution(mesh):
    field = P("chan", "group", None, None)
    in_specs = (
        field, field, field, P("chan", None), P("chan"), P("chan"), P("chan", None), P("chan"), P("chan"),
    )
    return jax.shard_map(
        shards, mesh=mesh, in_specs=in_specs, out_specs=(field, field, field), check_vma=False
    )
```
